32 devices in a mesh: dp: 8 (over z, x), tensor: 4 (over y, core).
Axes of the slice: x: 2, y: 2, z: 4, core: 2. Of those that a mesh axis runs over, the one named last changes fastest.
Arguments:
- block_input: bfloat16 [8192, 1536], P(('dp', 'tensor')), may hold values from -6 to 6
- gain_attention: float32 [1536], replicated, may hold values from 0.1 to 1.9
- gain_feedforward: float32 [1536], replicated, may hold values from 0.1 to 1.9
- w_query: bfloat16 [1536, 1536], P(None, 'tensor'), as said below
- w_key: bfloat16 [1536, 768], P(None, 'tensor'), as said below
- w_value: bfloat16 [1536, 768], P(None, 'tensor'), may hold values from -0.15625 to 0.15625
- w_output: bfloat16 [1536, 1536], P('tensor'), may hold values from -1.25 to 1.25
- w_gate: bfloat16 [1536, 4096], P(None, 'tensor'), may hold values from -0.15625 to 0.15625
- w_up: bfloat16 [1536, 4096], P(None, 'tensor'), may hold values from -0.15625 to 0.15625
- w_down: bfloat16 [4096, 1536], P('tensor'), may hold values from -0.09375 to 0.09375
- cotangent: bfloat16 [8192, 1536], P(('dp', 'tensor')), may hold values from -12 to 12
Outputs:
- block_output: bfloat16 [8192, 1536], P(('dp', 'tensor'))
- input_grad: bfloat16 [8192, 1536], P(('dp', 'tensor'))
- grad_gain_attention: float32 [1536], replicated
- grad_gain_feedforward: float32 [1536], replicated
- grad_query: float32 [1536, 1536], P(None, 'tensor')
- grad_key: float32 [1536, 768], P(None, 'tensor')
- grad_value: float32 [1536, 768], P(None, 'tensor')
- grad_output: float32 [1536, 1536], P('tensor')
- grad_gate: float32 [1536, 4096], P(None, 'tensor')
- grad_up: float32 [1536, 4096], P(None, 'tensor')
- grad_down: float32 [4096, 1536], P('tensor')
The draws below stay inside these ranges and needn't reach their ends.
Inputs may be any that keep to these rules, and one draw needn't show every extreme that they name: `w_query`: query projection. `w_key`: key projection with entries of order 1536^-0.5.
All inputs are finite; a program needn't handle non-finite values.
Results may differ from the reference program's by a relative error of at most 0.02.
Values may be sent and summed in bfloat16 or wider, within the bound.
No kernel may reach another device: no remote copies, remote signals or barrier semaphores. Data moves between devices by JAX's collectives and lax.ppermute only.
A program may use at most 192 MiB of HBM per device.

```python
import jax
import jax.numpy as jnp
from jax import lax

D = 1536
H = 16
KV = 8
HD = 96
FF = 4096
L = 1024
TOKENS = 8192


def key_columns(key):
    normal_draw = jax.random.normal(jax.random.fold_in(key, 7), (D, KV * HD), jnp.float32)
    return jnp.clip(normal_draw, -4.0, 4.0) * D ** (-0.5)


def draw_w_key(key, part):
    return key_columns(key).astype(jnp.bfloat16)


def draw_w_query(key, part):
    normal_draw = jax.random.normal(jax.random.fold_in(key, 11), (D, H * HD), jnp.float32)
    noise = jnp.clip(normal_draw, -4.0, 4.0) * D ** (-0.5)
    return noise.astype(jnp.bfloat16)


def draw_cotangent(key, part):
    rising = 1.0 + 2.0 * jnp.arange(TOKENS, dtype=jnp.float32)[:, None] / (TOKENS - 1)
    normal_draw = jax.random.normal(jax.random.fold_in(key, 3), (TOKENS, D), jnp.float32)
    return (jnp.clip(normal_draw, -4.0, 4.0) * rising).astype(jnp.bfloat16)


def steps_of(rng, shape, cuts, smallest, largest):
    level, own = 1.0, jax.random.fold_in(rng, 6)
    for dim, shards_of in cuts:
        heights = jnp.exp(jax.random.uniform(jax.random.fold_in(own, dim), (shards_of,), jnp.float32, smallest / len(cuts), largest / len(cuts)))
        level = level * jnp.repeat(heights, shape[dim] // shards_of).reshape([-1 if axis == dim else 1 for axis in range(len(shape))])
    return level


def scatter_about(stream_key, shape, scale, bound, split=(), kind=jnp.bfloat16):
    factor_of = steps_of(stream_key, shape, split, -0.22, 0.18) if split else 1.0
    drawn = jax.random.normal(stream_key, shape, jnp.float32) * scale * factor_of
    return jnp.minimum(jnp.maximum(drawn, -bound), bound).astype(kind)


def setup_inputs(seed: int = 0) -> dict:
    splits = jax.random.split(jax.random.key(seed), 12)
    block_input = scatter_about(splits[0], (TOKENS, D), 1.0, 6.0, ((0, 32),))
    gain_attention = jnp.clip(1.0 + 0.18 * jax.random.normal(splits[1], (D,), jnp.float32), 0.1, 1.9)
    gain_feedforward = jnp.clip(1.0 + 0.18 * jax.random.normal(splits[2], (D,), jnp.float32), 0.1, 1.9)
    w_query = draw_w_query(jax.random.fold_in(splits[11], 71), 0)
    w_key = draw_w_key(jax.random.fold_in(splits[11], 71), 0)
    w_value = scatter_about(splits[5], (D, KV * HD), D ** -0.5, 0.15625, ((1, 4),))
    w_output = scatter_about(splits[6], (H * HD, D), (H * HD * 16 // L) ** -0.5, 1.25, ((0, 4),))
    w_gate = scatter_about(splits[7], (D, FF), D ** -0.5, 0.15625, ((1, 4),))
    w_up = scatter_about(splits[8], (D, FF), D ** -0.5, 0.15625, ((1, 4),))
    w_down = scatter_about(splits[9], (FF, D), FF ** -0.5, 0.09375, ((0, 4),))
    cotangent = draw_cotangent(jax.random.fold_in(splits[11], 71), 0)
    return dict(block_input=block_input, gain_attention=gain_attention, gain_feedforward=gain_feedforward, w_query=w_query, w_key=w_key, w_value=w_value, w_output=w_output, w_gate=w_gate, w_up=w_up, w_down=w_down, cotangent=cotangent)


EPS = 1e-05
THETA = 100000.0

def rope_tables(length, width):
    position = jnp.arange(length, dtype=jnp.float32)[:, None]
    inverse = THETA ** (-jnp.arange(0, width, 2, dtype=jnp.float32) / width)
    angles = position * inverse[None, :]
    angles = jnp.concatenate([angles, angles], axis=-1)
    return (jnp.cos(angles), jnp.sin(angles))

def rotate(values_in, cosine, sine):
    half_width = values_in.shape[-1] // 2
    turned = jnp.concatenate([-values_in[..., half_width:], values_in[..., :half_width]], axis=-1)
    return values_in * cosine[:, None, :] + turned * sine[:, None, :]

def unrotate(grad_in, cosine, sine):
    half_width = grad_in.shape[-1] // 2
    scaled = grad_in * sine[:, None, :]
    turned = jnp.concatenate([scaled[..., half_width:], -scaled[..., :half_width]], axis=-1)
    return grad_in * cosine[:, None, :] + turned

def norm_forward(inputs, gain):
    recip = lax.rsqrt(lax.optimization_barrier(jnp.mean(inputs * inputs, axis=-1, keepdims=True)) + EPS)
    return ((inputs * recip * gain).astype(jnp.bfloat16), recip)

def norm_backward(inputs, recip, gain, dnormed):
    scaled = gain * dnormed
    gain_part = lax.optimization_barrier(jnp.sum(dnormed * inputs * recip, axis=0))
    inner = lax.optimization_barrier(jnp.mean(scaled * inputs, axis=-1, keepdims=True))
    return (gain_part, recip * scaled - inputs * recip * recip * recip * inner)

def masked_scores(query, keys, scale):
    length = query.shape[0]
    scores = jnp.einsum('lkgd,mkd->kglm', query.astype(jnp.float32), keys.astype(jnp.float32)) * scale
    causal = jnp.arange(length)[:, None] >= jnp.arange(length)[None, :]
    return jnp.where(causal, scores, -jnp.inf)

def attend(query, keys, values, scale):
    scores = masked_scores(query, keys, scale)
    row_max = lax.optimization_barrier(jnp.max(scores, axis=-1, keepdims=True))
    exponent = jnp.exp(scores - row_max)
    row_total = lax.optimization_barrier(jnp.sum(exponent, axis=-1, keepdims=True))
    probability = (exponent / row_total).astype(jnp.bfloat16)
    log_total = row_max + jnp.log(row_total)
    attended = jnp.einsum('kglm,mkd->lkgd', probability.astype(jnp.float32), values.astype(jnp.float32))
    return (attended.astype(jnp.bfloat16), log_total)

def attend_back(query, keys, values, attended, log_total, dattended, scale):
    scores = masked_scores(query, keys, scale)
    probability = jnp.exp(scores - log_total)
    prob_rounded = probability.astype(jnp.bfloat16).astype(jnp.float32)
    dattended32 = dattended.astype(jnp.float32)
    value_grad = jnp.einsum('kglm,lkgd->mkd', prob_rounded, dattended32)
    dprob = jnp.einsum('lkgd,mkd->kglm', dattended32, values.astype(jnp.float32))
    delta = lax.optimization_barrier(jnp.sum(dattended32 * attended.astype(jnp.float32), axis=-1))
    delta = jnp.transpose(delta, (1, 2, 0))[..., None]
    dscore = (probability * (dprob - delta)).astype(jnp.bfloat16).astype(jnp.float32)
    query_grad = jnp.einsum('kglm,mkd->lkgd', dscore, keys.astype(jnp.float32)) * scale
    key_grad = jnp.einsum('kglm,lkgd->mkd', dscore, query.astype(jnp.float32)) * scale
    return (query_grad, key_grad, value_grad)

def layer_sequence(members, weights):
    block_seq, grad_seq = members
    gain_attention, gain_feedforward, w_query, w_key, w_value, w_output, w_gate, w_up, w_down = weights
    scale = HD ** (-0.5)
    inputs = block_seq.astype(jnp.float32)
    normed_one, recip_one = norm_forward(inputs, gain_attention)
    cosine, sine = rope_tables(L, HD)
    query = rotate(jnp.dot(normed_one, w_query, preferred_element_type=jnp.float32).reshape(L, H, HD), cosine, sine)
    query = query.astype(jnp.bfloat16).reshape(L, KV, 2, HD)
    keys = rotate(jnp.dot(normed_one, w_key, preferred_element_type=jnp.float32).reshape(L, KV, HD), cosine, sine)
    keys = keys.astype(jnp.bfloat16)
    values = jnp.dot(normed_one, w_value, preferred_element_type=jnp.float32).astype(jnp.bfloat16).reshape(L, KV, HD)
    attended, log_total = attend(query, keys, values, scale)
    flat_attended = attended.reshape(L, H * HD)
    resid = inputs + jnp.dot(flat_attended, w_output, preferred_element_type=jnp.float32)
    normed_two, recip_two = norm_forward(resid, gain_feedforward)
    gate = jnp.dot(normed_two, w_gate, preferred_element_type=jnp.float32)
    up_proj = jnp.dot(normed_two, w_up, preferred_element_type=jnp.float32)
    sigmoid_gate = jax.nn.sigmoid(gate)
    activated = gate * sigmoid_gate
    hidden = (activated * up_proj).astype(jnp.bfloat16)
    output = (resid + jnp.dot(hidden, w_down, preferred_element_type=jnp.float32)).astype(jnp.bfloat16)
    grad_down = jnp.dot(hidden.T, grad_seq, preferred_element_type=jnp.float32)
    dhidden = jnp.dot(grad_seq, w_down.T, preferred_element_type=jnp.float32)
    dgate = (dhidden * up_proj * sigmoid_gate * (1.0 + gate * (1.0 - sigmoid_gate))).astype(jnp.bfloat16)
    dup_proj = (dhidden * activated).astype(jnp.bfloat16)
    grad_gate = jnp.dot(normed_two.T, dgate, preferred_element_type=jnp.float32)
    grad_up = jnp.dot(normed_two.T, dup_proj, preferred_element_type=jnp.float32)
    dnormed_two = jnp.dot(dgate, w_gate.T, preferred_element_type=jnp.float32) + jnp.dot(dup_proj, w_up.T, preferred_element_type=jnp.float32)
    gain_two_part, dresid_norm = norm_backward(resid, recip_two, gain_feedforward, dnormed_two)
    dresid = grad_seq.astype(jnp.float32) + dresid_norm
    dresid_bf = dresid.astype(jnp.bfloat16)
    grad_output = jnp.dot(flat_attended.T, dresid_bf, preferred_element_type=jnp.float32)
    dattended = jnp.dot(dresid_bf, w_output.T, preferred_element_type=jnp.float32).astype(jnp.bfloat16).reshape(L, KV, 2, HD)
    query_grad, key_grad, value_grad = attend_back(query, keys, values, attended, log_total, dattended, scale)
    query_grad = unrotate(query_grad.reshape(L, H, HD), cosine, sine).astype(jnp.bfloat16).reshape(L, H * HD)
    key_grad = unrotate(key_grad, cosine, sine).astype(jnp.bfloat16).reshape(L, KV * HD)
    value_grad = value_grad.astype(jnp.bfloat16).reshape(L, KV * HD)
    grad_query = jnp.dot(normed_one.T, query_grad, preferred_element_type=jnp.float32)
    grad_key = jnp.dot(normed_one.T, key_grad, preferred_element_type=jnp.float32)
    grad_value = jnp.dot(normed_one.T, value_grad, preferred_element_type=jnp.float32)
    dnormed_one = jnp.dot(query_grad, w_query.T, preferred_element_type=jnp.float32)
    dnormed_one = dnormed_one + jnp.dot(key_grad, w_key.T, preferred_element_type=jnp.float32)
    dnormed_one = dnormed_one + jnp.dot(value_grad, w_value.T, preferred_element_type=jnp.float32)
    gain_one_part, dinput_norm = norm_backward(inputs, recip_one, gain_attention, dnormed_one)
    input_grad = (dresid + dinput_norm).astype(jnp.bfloat16)
    grads = (gain_one_part, gain_two_part, grad_query, grad_key, grad_value, grad_output, grad_gate, grad_up, grad_down)
    return (output, input_grad, grads)

def reference(block_input, gain_attention, gain_feedforward, w_query, w_key, w_value, w_output, w_gate, w_up, w_down, cotangent):
    weights = (gain_attention, gain_feedforward, w_query, w_key, w_value, w_output, w_gate, w_up, w_down)
    sequences = TOKENS // L
    zero_grads = (jnp.zeros((D,), jnp.float32), jnp.zeros((D,), jnp.float32), jnp.zeros((D, H * HD), jnp.float32), jnp.zeros((D, KV * HD), jnp.float32), jnp.zeros((D, KV * HD), jnp.float32), jnp.zeros((H * HD, D), jnp.float32), jnp.zeros((D, FF), jnp.float32), jnp.zeros((D, FF), jnp.float32), jnp.zeros((FF, D), jnp.float32))

    def advance(carry, members):
        output, input_grad, grads = layer_sequence(members, weights)
        return (jax.tree.map(lambda left, right: left + right, carry, grads), (output, input_grad))
    totals, (outputs, input_grads) = lax.scan(advance, zero_grads, (block_input.reshape(sequences, L, D), cotangent.reshape(sequences, L, D)))
    block_output = outputs.reshape(TOKENS, D)
    input_grad = input_grads.reshape(TOKENS, D)
    return (block_output, input_grad, totals[0], totals[1], totals[2], totals[3], totals[4], totals[5], totals[6], totals[7], totals[8])
```

```python
import jax
import jax.numpy as jnp
from jax import lax
from jax.sharding import PartitionSpec as P

HD = 96
L = 1024

EPS = 1e-05
THETA = 100000.0


def rope_tables(position, width):
    inverse = THETA ** (-jnp.arange(0, width, 2, dtype=jnp.float32) / width)
    angles = position.astype(jnp.float32)[:, None] * inverse[None, :]
    angles = jnp.concatenate([angles, angles], axis=-1)
    return (jnp.cos(angles), jnp.sin(angles))


def rotate(values_in, cosine, sine):
    half_width = values_in.shape[-1] // 2
    turned = jnp.concatenate([-values_in[..., half_width:], values_in[..., :half_width]], axis=-1)
    return values_in * cosine[:, None, :] + turned * sine[:, None, :]


def unrotate(grad_in, cosine, sine):
    half_width = grad_in.shape[-1] // 2
    scaled = grad_in * sine[:, None, :]
    turned = jnp.concatenate([scaled[..., half_width:], -scaled[..., :half_width]], axis=-1)
    return grad_in * cosine[:, None, :] + turned


def norm_forward(inputs, gain):
    recip = lax.rsqrt(jnp.mean(inputs * inputs, axis=-1, keepdims=True) + EPS)
    return ((inputs * recip * gain).astype(jnp.bfloat16), recip)


def norm_backward(inputs, recip, gain, dnormed):
    scaled = gain * dnormed
    gain_part = jnp.sum(dnormed * inputs * recip, axis=0)
    inner = jnp.mean(scaled * inputs, axis=-1, keepdims=True)
    return (gain_part, recip * scaled - inputs * recip * recip * recip * inner)


def outer_sum(left, right):
    return lax.dot_general(
        left, right, (((0,), (0,)), ((), ())), preferred_element_type=jnp.float32
    )


def times_transpose(left, weight):
    return lax.dot_general(
        left, weight, (((1,), (1,)), ((), ())), preferred_element_type=jnp.float32
    )


def masked_scores(query, keys, mask):
    scores = jnp.einsum("lkgd,mkd->kglm", query, keys, preferred_element_type=jnp.float32) * HD ** (
        -0.5
    )
    return jnp.where(mask, scores, -jnp.inf)


def attend(query, keys, values, mask):
    scores = masked_scores(query, keys, mask)
    row_max = jnp.max(scores, axis=-1, keepdims=True)
    exponent = jnp.exp(scores - row_max)
    row_total = jnp.sum(exponent, axis=-1, keepdims=True)
    probability = (exponent / row_total).astype(jnp.bfloat16)
    log_total = row_max + jnp.log(row_total)
    attended = jnp.einsum("kglm,mkd->lkgd", probability, values, preferred_element_type=jnp.float32)
    return (attended.astype(jnp.bfloat16), log_total)


def attend_back(query, keys, values, attended, log_total, dattended, mask):
    scores = masked_scores(query, keys, mask)
    probability = jnp.exp(scores - log_total)
    prob_rounded = probability.astype(jnp.bfloat16)
    value_grad = jnp.einsum(
        "kglm,lkgd->mkd", prob_rounded, dattended, preferred_element_type=jnp.float32
    )
    dprob = jnp.einsum("lkgd,mkd->kglm", dattended, values, preferred_element_type=jnp.float32)
    delta = jnp.sum(dattended.astype(jnp.float32) * attended.astype(jnp.float32), axis=-1)
    delta = jnp.transpose(delta, (1, 2, 0))[..., None]
    dscore = (probability * (dprob - delta)).astype(jnp.bfloat16)
    query_grad = jnp.einsum(
        "kglm,mkd->lkgd", dscore, keys, preferred_element_type=jnp.float32
    ) * HD ** (-0.5)
    key_grad = jnp.einsum(
        "kglm,lkgd->mkd", dscore, query, preferred_element_type=jnp.float32
    ) * HD ** (-0.5)
    return (query_grad, key_grad, value_grad)


def swap(value, axis, size, bit):
    return lax.ppermute(value, axis, [(i, i ^ bit) for i in range(size)])


def gather_blocks(block, size):
    blocks = [block]
    for j in range(1, size):
        low = j & -j
        blocks.append(swap(blocks[j ^ low], "tensor", size, low))
    return blocks


def scatter_blocks(parts, size):
    bit = 1
    while bit < size:
        halves = {}
        for j in reversed(range(0, size, 2 * bit)):
            sent = swap(parts[j ^ bit].astype(jnp.bfloat16), "tensor", size, bit)
            halves[j] = parts[j].astype(jnp.float32) + sent.astype(jnp.float32)
        parts = halves
        bit *= 2
    return parts[0]


def after(value, *others):
    return lax.optimization_barrier((value, *others))[0]


def ring_order(size):
    return list(range(0, size, 2)) + list(reversed(range(1, size, 2)))


def ring_sum(streams, size):
    if size > 8:
        summed = lax.psum(tuple(array.astype(jnp.bfloat16) for array, _ in streams), "dp")
        return [total.astype(jnp.float32) for total in summed]
    order = ring_order(size)
    place = [0] * size
    for index, member in enumerate(order):
        place[member] = index
    place = jnp.array(place, jnp.int32)[lax.axis_index("dp")]
    pairs = {
        sign: [(order[i], order[(i + sign) % size]) for i in range(size)] for sign in (1, -1)
    }

    def piece(array, step):
        rows = array.shape[0] // size
        start = lax.rem(place + step + 4 * size, size) * rows
        return lax.dynamic_slice(array, (start, 0), (rows, array.shape[1]))

    held = [piece(array, -sign).astype(jnp.bfloat16) for array, sign in streams]
    for step in range(1, size):
        for k, (array, sign) in enumerate(streams):
            moved = lax.ppermute(held[k], "dp", pairs[sign])
            mine = piece(array, -sign * (1 + step)).astype(jnp.float32)
            held[k] = (moved.astype(jnp.float32) + mine).astype(jnp.bfloat16)
    totals = [jnp.zeros(array.shape, jnp.float32) for array, _ in streams]

    def put(k, value, step):
        array = streams[k][0]
        rows = array.shape[0] // size
        start = lax.rem(place + step + 4 * size, size) * rows
        totals[k] = lax.dynamic_update_slice(totals[k], value.astype(jnp.float32), (start, 0))

    for k in range(len(streams)):
        put(k, held[k], 0)
    for step in range(1, size):
        for k, (_, sign) in enumerate(streams):
            held[k] = lax.ppermute(held[k], "dp", pairs[sign])
            put(k, held[k], -sign * step)
    return totals


def cross_sum(value, size, axis):
    if size & (size - 1) == 0:
        bit = 1
        while bit < size:
            value = value + swap(value, axis, size, bit)
            bit *= 2
        return value
    return lax.psum(value, axis)


def make_body(dp, tensor):
    def body(
        block_input,
        gain_attention,
        gain_feedforward,
        w_query,
        w_key,
        w_value,
        w_output,
        w_gate,
        w_up,
        w_down,
        cotangent,
    ):
        query_cols = w_query.shape[1]
        pair_cols = w_key.shape[1]
        query_heads = query_cols // HD
        pair_heads = pair_cols // HD
        width = block_input.shape[1]
        hidden_cols = w_gate.shape[1]
        rows = block_input.shape[0]
        rows_all = rows * tensor
        me = lax.axis_index("tensor")
        row = jnp.concatenate(
            [(me ^ j) * rows + jnp.arange(rows, dtype=jnp.int32) for j in range(tensor)]
        )
        position = lax.rem(row, L)
        sequence = lax.div(row, L)
        mask = (row[:, None] >= row[None, :]) & (sequence[:, None] == sequence[None, :])
        cosine, sine = rope_tables(position, HD)

        inputs = block_input.astype(jnp.float32)
        normed_one, recip_one = norm_forward(inputs, gain_attention)
        full_one = jnp.concatenate(gather_blocks(normed_one, tensor), axis=0)
        full_grad = jnp.concatenate(gather_blocks(after(cotangent, full_one), tensor), axis=0)
        query = jnp.dot(full_one, w_query, preferred_element_type=jnp.float32).reshape(
            rows_all, query_heads, HD
        )
        query = rotate(query, cosine, sine).astype(jnp.bfloat16)
        query = query.reshape(rows_all, pair_heads, 2, HD)
        keys = jnp.dot(full_one, w_key, preferred_element_type=jnp.float32).reshape(
            rows_all, pair_heads, HD
        )
        keys = rotate(keys, cosine, sine).astype(jnp.bfloat16)
        values = (
            jnp.dot(full_one, w_value, preferred_element_type=jnp.float32)
            .astype(jnp.bfloat16)
            .reshape(rows_all, pair_heads, HD)
        )
        attended, log_total = attend(query, keys, values, mask)
        flat_attended = attended.reshape(rows_all, query_cols)

        def blocks_of(array):
            return [array[j * rows : (j + 1) * rows] for j in range(tensor)]

        resid = inputs + scatter_blocks(
            blocks_of(jnp.dot(flat_attended, w_output, preferred_element_type=jnp.float32)), tensor
        )
        normed_two, recip_two = norm_forward(resid, gain_feedforward)
        full_two = jnp.concatenate(gather_blocks(normed_two, tensor), axis=0)
        gate = jnp.dot(full_two, w_gate, preferred_element_type=jnp.float32)
        up_proj = jnp.dot(full_two, w_up, preferred_element_type=jnp.float32)
        sigmoid_gate = jax.nn.sigmoid(gate)
        activated = gate * sigmoid_gate
        hidden = (activated * up_proj).astype(jnp.bfloat16)
        grad_down = outer_sum(hidden, full_grad)
        dhidden = times_transpose(full_grad, w_down)
        dgate = (dhidden * up_proj * sigmoid_gate * (1.0 + gate * (1.0 - sigmoid_gate))).astype(
            jnp.bfloat16
        )
        dup_proj = (dhidden * activated).astype(jnp.bfloat16)
        grad_gate = outer_sum(full_two, dgate)
        grad_up = outer_sum(full_two, dup_proj)
        half = width // 2
        down_a, down_b, total_gate, total_up = ring_sum(
            [(grad_down[:, :half], 1), (grad_down[:, half:], -1), (grad_gate, 1), (grad_up, -1)],
            dp,
        )
        dnormed_two = scatter_blocks(
            blocks_of(times_transpose(dgate, w_gate) + times_transpose(dup_proj, w_up)), tensor
        )
        gain_two_part, dresid_norm = norm_backward(resid, recip_two, gain_feedforward, dnormed_two)
        dresid = cotangent.astype(jnp.float32) + dresid_norm
        full_dresid = jnp.concatenate(gather_blocks(dresid.astype(jnp.bfloat16), tensor), axis=0)
        late_hidden = after(hidden, full_dresid)
        block_output = (
            resid
            + scatter_blocks(
                blocks_of(jnp.dot(late_hidden, w_down, preferred_element_type=jnp.float32)), tensor
            )
        ).astype(jnp.bfloat16)
        grad_output = outer_sum(flat_attended, full_dresid)
        dattended = (
            times_transpose(full_dresid, w_output)
            .astype(jnp.bfloat16)
            .reshape(rows_all, pair_heads, 2, HD)
        )
        query_grad, key_grad, value_grad = attend_back(
            query, keys, values, attended, log_total, dattended, mask
        )
        query_grad = (
            unrotate(query_grad.reshape(rows_all, query_heads, HD), cosine, sine)
            .astype(jnp.bfloat16)
            .reshape(rows_all, query_cols)
        )
        key_grad = (
            unrotate(key_grad, cosine, sine).astype(jnp.bfloat16).reshape(rows_all, pair_cols)
        )
        value_grad = value_grad.astype(jnp.bfloat16).reshape(rows_all, pair_cols)
        both_grad = jnp.concatenate([key_grad, value_grad], axis=1)
        grad_query = outer_sum(full_one, query_grad)
        grad_both = outer_sum(full_one, both_grad)
        out_a, out_b, total_query, total_both = ring_sum(
            [
                (grad_output[:, :half], 1),
                (grad_output[:, half:], -1),
                (grad_query, 1),
                (grad_both, -1),
            ],
            dp,
        )
        term = times_transpose(query_grad, w_query)
        term = term + times_transpose(key_grad, w_key)
        dnormed_one = scatter_blocks(blocks_of(term + times_transpose(value_grad, w_value)), tensor)
        gain_one_part, dinput_norm = norm_backward(inputs, recip_one, gain_attention, dnormed_one)
        input_grad = (dresid + dinput_norm).astype(jnp.bfloat16)
        parts = jnp.stack([gain_one_part, gain_two_part])
        gains = cross_sum(cross_sum(parts, tensor, "tensor"), dp, "dp")
        return (
            block_output,
            input_grad,
            gains[0],
            gains[1],
            total_query,
            total_both[:, :pair_cols],
            total_both[:, pair_cols:],
            jnp.concatenate([out_a, out_b], axis=1),
            total_gate,
            total_up,
            jnp.concatenate([down_a, down_b], axis=1),
        )

    return body


def solution(mesh):
    placed = (
        P(("dp", "tensor"), None),
        P(),
        P(),
        P(None, "tensor"),
        P(None, "tensor"),
        P(None, "tensor"),
        P("tensor", None),
        P(None, "tensor"),
        P(None, "tensor"),
        P("tensor", None),
        P(("dp", "tensor"), None),
    )
    return jax.shard_map(
        make_body(mesh.shape["dp"], mesh.shape["tensor"]),
        mesh=mesh,
        in_specs=placed,
        out_specs=(
            P(("dp", "tensor"), None),
            P(("dp", "tensor"), None),
            P(),
            P(),
            P(None, "tensor"),
            P(None, "tensor"),
            P(None, "tensor"),
            P("tensor", None),
            P(None, "tensor"),
            P(None, "tensor"),
            P("tensor", None),
        ),
        check_vma=False,
    )
```

```python
import functools

import jax
import jax.numpy as jnp
from jax import lax
from jax.experimental import pallas as pl
from jax.experimental.pallas import tpu as pltpu
from jax.sharding import PartitionSpec as P


HD = 96
L = 1024
LANES = 128

EPS = 1e-05
THETA = 100000.0


def rope_tables(rows):
    half = HD // 2
    position = (jnp.arange(rows, dtype=jnp.int32) % L).astype(jnp.float32)[:, None]
    inverse = THETA ** (-jnp.arange(0, HD, 2, dtype=jnp.float32) / HD)
    angles = position * inverse[None, :]
    pad = ((0, 0), (0, LANES // 2 - half))
    cosine, sine = jnp.pad(jnp.cos(angles), pad), jnp.pad(jnp.sin(angles), pad)
    return (
        jnp.concatenate([cosine, cosine], axis=1),
        jnp.concatenate([-sine, sine], axis=1),
    )


def pad_halves(weight):
    split = weight.reshape(weight.shape[0], -1, 2, HD // 2)
    split = jnp.pad(split, ((0, 0), (0, 0), (0, 0), (0, LANES // 2 - HD // 2)))
    return split.reshape(weight.shape[0], -1)


def pad_heads(weight):
    split = weight.reshape(weight.shape[0], -1, HD)
    return jnp.pad(split, ((0, 0), (0, 0), (0, LANES - HD))).reshape(weight.shape[0], -1)


def pad_head_rows(weight):
    split = weight.reshape(-1, HD, weight.shape[1])
    return jnp.pad(split, ((0, 0), (0, LANES - HD), (0, 0))).reshape(-1, weight.shape[1])


def selection(columns, head, halves):
    lane = lax.broadcasted_iota(jnp.int32, (LANES, columns), 0)
    column = lax.broadcasted_iota(jnp.int32, (LANES, columns), 1)
    if halves:
        wide, half = LANES // 2, HD // 2
        upper = lane >= wide
        inner = jnp.where(upper, lane - wide, lane)
        target = jnp.where(inner < half, inner + jnp.where(upper, half, 0), -columns - LANES * 64)
    else:
        target = jnp.where(lane < HD, lane, -columns - LANES * 64)
    return jnp.where(target + head * HD == column, 1.0, 0.0).astype(jnp.bfloat16)


def dot(left, right, dims):
    return lax.dot_general(left, right, (dims, ((), ())), preferred_element_type=jnp.float32)


NN, NT, TN = ((1,), (0,)), ((1,), (1,)), ((0,), (0,))


def whole(shape):
    return pl.BlockSpec(shape, lambda *_: (0,) * len(shape), pipeline_mode=pl.Buffered(1))


def params(mebibytes, grid=True):
    return pltpu.CompilerParams(
        dimension_semantics=("arbitrary",) if grid else None,
        vmem_limit_bytes=mebibytes * 1024 * 1024,
    )


def cost(flops, moved, exps=0):
    return pl.CostEstimate(flops=int(flops), bytes_accessed=int(moved), transcendentals=int(exps))


def softmax_block(query, keys, block, step, span):
    scores = dot(query, keys, NT) * HD ** (-0.5)
    row = lax.broadcasted_iota(jnp.int32, scores.shape, 0)
    row = jnp.where(row >= step, row - step, row) + block * step
    column = lax.broadcasted_iota(jnp.int32, scores.shape, 1) + span
    scores = jnp.where(row >= column, scores, -jnp.inf)
    exponent = jnp.exp(scores - jnp.max(scores, axis=1, keepdims=True))
    return exponent * (1.0 / jnp.sum(exponent, axis=1, keepdims=True))


def turn(value, cosine, sine):
    return value * cosine + pltpu.roll(value, LANES // 2, 1) * sine


def unturn(value, cosine, sine):
    return value * cosine + pltpu.roll(value * sine, LANES // 2, 1)


def attend_kernel(pairs, step, qkv, cosine, sine, heads_out, flat_out, q_out, k_out, v_out):
    rows = cosine.shape[0]
    cos, sin = cosine[...], sine[...]
    for h in range(2 * pairs):
        q_out[:, h * LANES : (h + 1) * LANES] = turn(
            qkv[:, h * LANES : (h + 1) * LANES], cos, sin
        ).astype(jnp.bfloat16)
    for g in range(pairs):
        at = (2 * pairs + g) * LANES
        k_out[:, g * LANES : (g + 1) * LANES] = turn(
            qkv[:, at : at + LANES], cos, sin
        ).astype(jnp.bfloat16)
    at = 3 * pairs * LANES
    v_out[...] = qkv[:, at : at + pairs * LANES].astype(jnp.bfloat16)
    for g in range(pairs):
        kv = slice(g * LANES, (g + 1) * LANES)
        for block in range(rows // step):
            here = slice(block * step, (block + 1) * step)
            start = (block * step) // L * L
            past = slice(start, (block + 1) * step)
            one, two = (slice((2 * g + e) * LANES, (2 * g + e + 1) * LANES) for e in range(2))
            query = jnp.concatenate([q_out[here, one], q_out[here, two]], axis=0)
            prob = softmax_block(query, k_out[past, kv], block, step, start).astype(jnp.bfloat16)
            result = dot(prob, v_out[past, kv], NN).astype(jnp.bfloat16)
            heads_out[here, one] = result[:step]
            heads_out[here, two] = result[step:]
    flat = sum(
        dot(heads_out[:, h * LANES : (h + 1) * LANES], selection(2 * pairs * HD, h, False), NN)
        for h in range(2 * pairs)
    )
    flat_out[...] = flat.astype(jnp.bfloat16)


def attend(qkv, cosine, sine, pairs, step):
    rows = qkv.shape[0]
    shapes = [2 * pairs * LANES, 2 * pairs * HD, 2 * pairs * LANES, pairs * LANES, pairs * LANES]
    area = rows * min(rows, L) * 2 * pairs * 5 // 8
    return pl.pallas_call(
        functools.partial(attend_kernel, pairs, step),
        out_shape=[jax.ShapeDtypeStruct((rows, c), jnp.bfloat16) for c in shapes],
        compiler_params=params(26, False),
        cost_estimate=cost(4 * area * LANES, 10 * qkv.size, area),
        name="attend",
    )(qkv, cosine, sine)


def attend_back_kernel(pairs, step, group, *refs):
    q, k, v, heads, dheads, cosine, sine = refs[:7]
    out, dk, dv, dq = refs[-4:]
    rows = cosine.shape[0]
    cos, sin = cosine[...], sine[...]
    scale = HD ** (-0.5)
    width = 2 * pairs * HD
    flat_q = jnp.zeros((rows, width), jnp.float32)
    flat_kv = jnp.zeros((rows, width), jnp.float32)
    if len(refs) > 11:
        flat_q += refs[7][:, :width].astype(jnp.float32)
        flat_kv += refs[7][:, width:].astype(jnp.float32)
    for g in (group,):
        kv = slice(g * LANES, (g + 1) * LANES)
        dk[...] = jnp.zeros_like(dk)
        dv[...] = jnp.zeros_like(dv)
        for block in range(rows // step):
            here = slice(block * step, (block + 1) * step)
            start = (block * step) // L * L
            past = slice(start, (block + 1) * step)
            one, two = (slice((2 * g + e) * LANES, (2 * g + e + 1) * LANES) for e in range(2))

            def both(ref):
                return jnp.concatenate([ref[here, one], ref[here, two]], axis=0)

            query, dhead = both(q), both(dheads)
            prob = softmax_block(query, k[past, kv], block, step, start)
            dv[past] += dot(prob.astype(jnp.bfloat16), dhead, TN)
            delta = jnp.sum(
                dhead.astype(jnp.float32) * both(heads).astype(jnp.float32), axis=1, keepdims=True
            )
            dscore = (prob * (dot(dhead, v[past, kv], NT) - delta)).astype(jnp.bfloat16)
            dk[past] += dot(dscore, query, TN)
            dquery = dot(dscore, k[past, kv], NN)
            dq[0, here] = dquery[:step]
            dq[1, here] = dquery[step:]
        for e in range(2):
            back = unturn(dq[e] * scale, cos, sin).astype(jnp.bfloat16)
            flat_q += dot(back, selection(width, 2 * g + e, True), NN)
        back = unturn(dk[...] * scale, cos, sin).astype(jnp.bfloat16)
        flat_kv += dot(back, selection(width, g, True), NN)
        flat_kv += dot(dv[...].astype(jnp.bfloat16), selection(width, pairs + g, False), NN)
    out[:, :width] = flat_q.astype(jnp.bfloat16)
    out[:, width:] = flat_kv.astype(jnp.bfloat16)


def attend_back(q, k, v, heads, dheads, cosine, sine, pairs, step, group, before):
    rows = q.shape[0]
    area = rows * min(rows, L) * 2 * 5 // 8
    held = [] if before is None else [before]
    return pl.pallas_call(
        functools.partial(attend_back_kernel, pairs, step, group),
        out_shape=jax.ShapeDtypeStruct((rows, 4 * pairs * HD), jnp.bfloat16),
        scratch_shapes=[
            pltpu.VMEM((rows, LANES), jnp.float32),
            pltpu.VMEM((rows, LANES), jnp.float32),
            pltpu.VMEM((2, rows, LANES), jnp.float32),
        ],
        compiler_params=params(26, False),
        cost_estimate=cost(10 * area * LANES, 10 * q.size, area),
        name="attend_back",
    )(q, k, v, heads, dheads, cosine, sine, *held)


def place_kernel(count, me, *refs):
    for k in range(count):

        @pl.when(pl.program_id(0) == k)
        def _(k=k):
            refs[count][...] = refs[k][...]


def place(blocks, me):
    rows, columns = blocks[0].shape
    count = len(blocks)
    return pl.pallas_call(
        functools.partial(place_kernel, count),
        out_shape=jax.ShapeDtypeStruct((count * rows, columns), blocks[0].dtype),
        grid_spec=pltpu.PrefetchScalarGridSpec(
            num_scalar_prefetch=1,
            grid=(count,),
            in_specs=[whole((rows, columns))] * count,
            out_specs=pl.BlockSpec((rows, columns), lambda s, m: (m[0] ^ s, 0)),
        ),
        compiler_params=params(12),
        cost_estimate=cost(0, 4 * count * rows * columns),
        name="place",
    )(me, *blocks)


def norm_place_kernel(count, me, gain, *refs):
    for k in range(count):

        @pl.when(pl.program_id(0) == k)
        def _(k=k):
            refs[count + 1][...] = refs[k][...]
            value = refs[k][...].astype(jnp.float32)
            recip = lax.rsqrt(jnp.mean(value * value, axis=-1, keepdims=True) + EPS)
            refs[count][...] = (value * recip * gain[...]).astype(jnp.bfloat16)


def norm_place(blocks, gain, me):
    rows, columns = blocks[0].shape
    count = len(blocks)
    spot = pl.BlockSpec((rows, columns), lambda s, m: (m[0] ^ s, 0))
    return pl.pallas_call(
        functools.partial(norm_place_kernel, count),
        out_shape=[jax.ShapeDtypeStruct((count * rows, columns), jnp.bfloat16)] * 2,
        grid_spec=pltpu.PrefetchScalarGridSpec(
            num_scalar_prefetch=1,
            grid=(count,),
            in_specs=[whole((1, columns))] + [whole((rows, columns))] * count,
            out_specs=[spot, spot],
        ),
        compiler_params=params(14),
        cost_estimate=cost(0, 6 * count * rows * columns),
        name="norm_place",
    )(me, gain[None, :], *blocks)


def project_kernel(count, me, inputs, gain, *refs):
    attended, weight, normed, own = refs[:count], *refs[count:]
    joined = jnp.concatenate([a[...] for a in attended], axis=1)
    value = inputs[...].astype(jnp.float32) + dot(joined, weight[...], NN)
    recip = lax.rsqrt(jnp.mean(value * value, axis=-1, keepdims=True) + EPS)
    normed[...] = (value * recip * gain[...]).astype(jnp.bfloat16)

    @pl.when(pl.program_id(0) == me[0])
    def _():
        own[...] = value


def project(inputs, gain, attended, weight, me):
    count = len(attended)
    rows_all, columns = inputs.shape
    rows = rows_all // count
    depth = attended[0].shape[1]
    mine = pl.BlockSpec((rows, columns), lambda s, m: (s, 0))
    return pl.pallas_call(
        functools.partial(project_kernel, count),
        out_shape=[
            jax.ShapeDtypeStruct((rows_all, columns), jnp.bfloat16),
            jax.ShapeDtypeStruct((rows, columns), jnp.float32),
        ],
        grid_spec=pltpu.PrefetchScalarGridSpec(
            num_scalar_prefetch=1,
            grid=(count,),
            in_specs=[mine, whole((1, columns))]
            + [pl.BlockSpec((rows, depth), lambda s, m: (s, 0))] * count
            + [whole(weight.shape)],
            out_specs=[mine, pl.BlockSpec((rows, columns), lambda s, m: (0, 0))],
        ),
        compiler_params=params(30),
        cost_estimate=cost(
            2 * rows_all * depth * count * columns, 6 * inputs.size + 2 * weight.size
        ),
        name="project",
    )(me, inputs, gain[None, :], *attended, weight)


def swap(value, axis, size, bit):
    return lax.ppermute(value, axis, [(i, i ^ bit) for i in range(size)])


def gather_blocks(block, size):
    blocks = [block]
    for j in range(1, size):
        low = j & -j
        blocks.append(swap(blocks[j ^ low], "tensor", size, low))
    return blocks


def gather_weight(weight, size, dp):
    far = size // 2
    blocks = {0: weight}
    if dp % 2 == 0 and size >= 4:
        half = weight.shape[0] // 2
        side = lax.axis_index("dp") & 1
        part = lax.dynamic_slice(weight, (side * half, 0), (half, weight.shape[1]))
        part = swap(part, "tensor", size, far)
        other = swap(part, "dp", dp, 1)
        first, second = jnp.where(side == 0, part, other), jnp.where(side == 0, other, part)
        blocks[far] = jnp.concatenate([first, second], axis=0)
    for j in range(1, size):
        if j not in blocks:
            low = j & -j
            blocks[j] = swap(blocks[j ^ low], "tensor", size, low)
    return jnp.concatenate([blocks[j] for j in range(size)], axis=0)


def scatter_sum(array, size, me):
    rows = array.shape[0] // size
    parts = {
        j: lax.dynamic_slice(array, ((me ^ j) * rows, 0), (rows, array.shape[1]))
        for j in range(size)
    }
    bit = 1
    while bit < size:
        halves = {}
        for j in reversed(range(0, size, 2 * bit)):
            sent = swap(parts[j ^ bit].astype(jnp.bfloat16), "tensor", size, bit)
            halves[j] = parts[j].astype(jnp.float32) + sent.astype(jnp.float32)
        parts = halves
        bit *= 2
    return parts[0]


def after(value, *others):
    return lax.optimization_barrier((value, *others))[0]


def ring_order(size):
    return list(range(0, size, 2)) + list(reversed(range(1, size, 2)))


def slices_of(main, side, size, width):
    spans = [(0, main[0] // size, c) for c in range(0, main[1], width)]
    spans += [(1, side[0] // size, c) for c in range(0, side[1] // 2, width)]
    return spans, sum(span[1] for span in spans)


def pack_kernel(spans, width, start, main, side, out):
    at = 0
    for which, rows, column in spans:
        out[at : at + rows] = (main, side)[which][:, column : column + width]
        at += rows


def pack(main, side, half, start, sign, width, size):
    spans, depth = slices_of(main.shape, side.shape, size, width)

    def chunk(s, m):
        return lax.rem(m[0] + 2 * size - sign * (1 + s), size)

    return pl.pallas_call(
        functools.partial(pack_kernel, spans, width),
        out_shape=jax.ShapeDtypeStruct((size * depth, width), jnp.bfloat16),
        grid_spec=pltpu.PrefetchScalarGridSpec(
            num_scalar_prefetch=1,
            grid=(size,),
            in_specs=[
                pl.BlockSpec((main.shape[0] // size, main.shape[1]), lambda s, m: (chunk(s, m), 0)),
                pl.BlockSpec(
                    (side.shape[0] // size, side.shape[1] // 2), lambda s, m: (chunk(s, m), half)
                ),
            ],
            out_specs=pl.BlockSpec((depth, width), lambda s, m: (s, 0)),
        ),
        compiler_params=params(8),
        cost_estimate=cost(0, 4 * size * depth * width),
        name="pack",
    )(start, main, side)


def unpack_kernel(spans, width, count, start, *refs):
    pieces, outs = refs[: 2 * count], refs[-3:]
    for k in range(2 * count):

        @pl.when(pl.program_id(0) == k)
        def _(k=k):
            way, at = k // count, 0
            for which, rows, column in spans[way]:
                target = outs[2] if which else outs[way]
                value = pieces[k][at : at + rows].astype(jnp.float32)
                target[:, column : column + width] = value
                at += rows


def unpack(pieces, shapes, start, first, totals, width, size):
    spans = [slices_of(shape, shapes[2], size, width) for shape in shapes[:2]]
    depth = spans[0][1]
    count = len(pieces) // 2

    def forward(s, m):
        step = jnp.minimum(s, count - 1) + first
        return (lax.rem(m[0] + size - step, size), 0)

    def backward(s, m):
        step = jnp.maximum(s - count, 0) + first
        return (lax.rem(m[0] + step, size), 0)

    def beside(s, m):
        turned = s >= count
        chunk = jnp.where(turned, m[0] + s - count + first, m[0] + size - s - first)
        return (lax.rem(chunk, size), jnp.where(turned, 1, 0))

    held = [] if totals is None else list(totals)
    (rows_a, cols_a), (rows_b, cols_b), (rows_c, cols_c) = shapes
    return pl.pallas_call(
        functools.partial(unpack_kernel, [span[0] for span in spans], width, count),
        out_shape=[jax.ShapeDtypeStruct(shape, jnp.float32) for shape in shapes],
        grid_spec=pltpu.PrefetchScalarGridSpec(
            num_scalar_prefetch=1,
            grid=(2 * count,),
            in_specs=[whole((depth, width))] * (2 * count)
            + [pl.BlockSpec(memory_space=pl.ANY)] * len(held),
            out_specs=[
                pl.BlockSpec((rows_a // size, cols_a), forward),
                pl.BlockSpec((rows_b // size, cols_b), backward),
                pl.BlockSpec((rows_c // size, cols_c // 2), beside),
            ],
        ),
        input_output_aliases={1 + 2 * count + k: k for k in range(len(held))},
        compiler_params=params(56),
        cost_estimate=cost(0, 12 * count * depth * width),
        name="unpack",
    )(start, *pieces, *held)


def ring_sum(first, second, side, width, size):
    if size > 8:
        summed = lax.psum((first, second, side), "dp")
        return [total.astype(jnp.float32) for total in summed]
    order = ring_order(size)
    position = [0] * size
    for index, member in enumerate(order):
        position[member] = index
    start = jnp.array(position, jnp.int32)[lax.axis_index("dp")][None]
    hops = {
        sign: [(order[i], order[(i + sign) % size]) for i in range(size)] for sign in (1, -1)
    }

    def hop(k, value):
        return lax.ppermute(value, "dp", hops[(1, -1)[k]])

    packed = [
        pack(main, side, k, start, (1, -1)[k], width, size) for k, main in enumerate((first, second))
    ]
    depth = packed[0].shape[0] // size
    held = [array[:depth] for array in packed]
    for step in range(1, size):
        for k in range(2):
            moved = hop(k, held[k]).astype(jnp.float32)
            mine = packed[k][step * depth : (step + 1) * depth].astype(jnp.float32)
            held[k] = (moved + mine).astype(jnp.bfloat16)
    pieces = [[held[0]], [held[1]]]
    for _ in range(1, size):
        for k in range(2):
            pieces[k].append(hop(k, pieces[k][-1]))
    shapes = (first.shape, second.shape, side.shape)
    totals, low = None, 0
    for high in sorted({size // 2, size - 2, size - 1, size} - {0}):
        if high > low:
            some = pieces[0][low:high] + pieces[1][low:high]
            totals = unpack(some, shapes, start, low, totals, width, size)
            low = high
    return totals


def cross_sum(value, size, axis):
    if size & (size - 1) == 0:
        bit = 1
        while bit < size:
            value = value + swap(value, axis, size, bit)
            bit *= 2
        return value
    return lax.psum(value, axis)


def norm_backward(inputs, gain, dnormed):
    recip = lax.rsqrt(jnp.mean(inputs * inputs, axis=-1, keepdims=True) + EPS)
    scaled = gain * dnormed
    gain_part = jnp.sum(dnormed * inputs * recip, axis=0)
    inner = jnp.mean(scaled * inputs, axis=-1, keepdims=True)
    return (gain_part, recip * scaled - inputs * recip * recip * recip * inner)


def make_body(dp, tensor):
    def layer(
        block_input,
        gain_attention,
        gain_feedforward,
        w_query,
        w_key,
        w_value,
        w_output,
        w_gate,
        w_up,
        w_down,
        cotangent,
    ):
        pair_cols = w_key.shape[1]
        pairs = pair_cols // HD
        rows = block_input.shape[0]
        step = 256
        me = lax.axis_index("tensor")
        spot = me[None].astype(jnp.int32)
        cosine, sine = rope_tables(rows * tensor)
        w_padded = jnp.concatenate(
            [pad_halves(w_query), pad_halves(w_key), pad_heads(w_value)], axis=1
        )
        w_both = jnp.concatenate([w_key.T, w_value.T], axis=0)
        w_output_padded = pad_head_rows(w_output)

        blocks = gather_blocks(block_input, tensor)
        full_one, full_inputs = norm_place(blocks, gain_attention, spot)
        weight = gather_weight(after(w_output, blocks[-1]), tensor, dp)
        qkv = dot(full_one, w_padded, NN)
        heads, flat, q, k, v = attend(qkv, cosine, sine, pairs, step)
        attended = gather_blocks(flat, tensor)
        full_two, resid = project(full_inputs, gain_feedforward, attended, weight, spot)
        full_grad = place(gather_blocks(after(cotangent, attended[-1]), tensor), spot)

        gate = dot(full_two, w_gate, NN)
        up_proj = dot(full_two, w_up, NN)
        sigmoid_gate = jax.nn.sigmoid(gate)
        activated = gate * sigmoid_gate
        hidden = (activated * up_proj).astype(jnp.bfloat16)
        grad_down = dot(hidden, full_grad, TN).astype(jnp.bfloat16)
        dhidden = dot(full_grad, w_down, NT)
        dgate = (dhidden * up_proj * sigmoid_gate * (1.0 + gate * (1.0 - sigmoid_gate))).astype(
            jnp.bfloat16
        )
        dup_proj = (dhidden * activated).astype(jnp.bfloat16)
        grad_gate = dot(full_two, dgate, TN).astype(jnp.bfloat16)
        grad_up = dot(full_two, dup_proj, TN).astype(jnp.bfloat16)
        total_gate, total_up, total_down = ring_sum(grad_gate, grad_up, grad_down, 256, dp)
        dgate, dup_proj = lax.optimization_barrier((dgate, dup_proj, grad_gate, grad_up, grad_down))[:2]
        dnormed_two = (dot(dgate, w_gate, NT) + dot(dup_proj, w_up, NT)).astype(jnp.bfloat16)
        dnormed_two = scatter_sum(dnormed_two, tensor, me)
        gain_two_part, dresid_norm = norm_backward(resid, gain_feedforward, dnormed_two)
        dresid = cotangent.astype(jnp.float32) + dresid_norm
        full_dresid = place(gather_blocks(dresid.astype(jnp.bfloat16), tensor), spot)
        late_hidden = after(hidden, full_dresid)
        block_output = (
            resid
            + scatter_sum(dot(late_hidden, w_down, NN).astype(jnp.bfloat16), tensor, me)
        ).astype(jnp.bfloat16)
        dheads = dot(full_dresid, w_output_padded, NT).astype(jnp.bfloat16)
        dqkv = None
        for group in range(pairs):
            dqkv = attend_back(
                q, k, v, heads, dheads, cosine, sine, pairs, step, group, dqkv
            )
        grad_output = dot(flat, full_dresid, TN).astype(jnp.bfloat16)
        dquery, dboth = dqkv[:, : 2 * pair_cols], dqkv[:, 2 * pair_cols :]
        grad_query = dot(full_one, dquery, TN).astype(jnp.bfloat16)
        grad_both = dot(dboth, full_one, TN).astype(jnp.bfloat16)
        total_query, total_both, total_output = ring_sum(
            grad_query, grad_both, grad_output, w_query.shape[1], dp
        )
        dnormed_one = scatter_sum(
            (dot(dquery, w_query, NT) + dot(dboth, w_both, NN)).astype(jnp.bfloat16), tensor, me
        )
        gain_one_part, dinput_norm = norm_backward(
            block_input.astype(jnp.float32), gain_attention, dnormed_one
        )
        input_grad = (dresid + dinput_norm).astype(jnp.bfloat16)
        gains = jnp.stack([gain_one_part, gain_two_part])
        gains = cross_sum(cross_sum(gains, tensor, "tensor"), dp, "dp")
        return (
            block_output,
            input_grad,
            gains[0],
            gains[1],
            total_query,
            total_both[:pair_cols].T,
            total_both[pair_cols:].T,
            total_output,
            total_gate,
            total_up,
            total_down,
        )

    return layer


def solution(mesh):
    placed = (
        P(("dp", "tensor"), None),
        P(),
        P(),
        P(None, "tensor"),
        P(None, "tensor"),
        P(None, "tensor"),
        P("tensor", None),
        P(None, "tensor"),
        P(None, "tensor"),
        P("tensor", None),
        P(("dp", "tensor"), None),
    )
    return jax.shard_map(
        make_body(mesh.shape["dp"], mesh.shape["tensor"]),
        mesh=mesh,
        in_specs=placed,
        out_specs=(
            P(("dp", "tensor"), None),
            P(("dp", "tensor"), None),
            P(),
            P(),
            P(None, "tensor"),
            P(None, "tensor"),
            P(None, "tensor"),
            P("tensor", None),
            P(None, "tensor"),
            P(None, "tensor"),
            P("tensor", None),
        ),
        check_vma=False,
    )
```

```python
import functools

import jax
import jax.numpy as jnp
from jax import lax
from jax.experimental import pallas as pl
from jax.experimental.pallas import tpu as pltpu
from jax.sharding import PartitionSpec as P


HD = 96
L = 1024
LANES = 128

EPS = 1e-05
THETA = 100000.0


def rope_tables(rows):
    half = HD // 2
    position = (jnp.arange(rows, dtype=jnp.int32) % L).astype(jnp.float32)[:, None]
    inverse = THETA ** (-jnp.arange(0, HD, 2, dtype=jnp.float32) / HD)
    angles = position * inverse[None, :]
    pad = ((0, 0), (0, LANES // 2 - half))
    cosine, sine = jnp.pad(jnp.cos(angles), pad), jnp.pad(jnp.sin(angles), pad)
    return (
        jnp.concatenate([cosine, cosine], axis=1),
        jnp.concatenate([-sine, sine], axis=1),
    )


def pad_halves(weight):
    split = weight.reshape(weight.shape[0], -1, 2, HD // 2)
    split = jnp.pad(split, ((0, 0), (0, 0), (0, 0), (0, LANES // 2 - HD // 2)))
    return split.reshape(weight.shape[0], -1)


def pad_heads(weight):
    split = weight.reshape(weight.shape[0], -1, HD)
    return jnp.pad(split, ((0, 0), (0, 0), (0, LANES - HD))).reshape(weight.shape[0], -1)


def pad_head_rows(weight):
    split = weight.reshape(-1, HD, weight.shape[1])
    return jnp.pad(split, ((0, 0), (0, LANES - HD), (0, 0))).reshape(-1, weight.shape[1])


def selection(columns, head, halves):
    lane = lax.broadcasted_iota(jnp.int32, (LANES, columns), 0)
    column = lax.broadcasted_iota(jnp.int32, (LANES, columns), 1)
    if halves:
        wide, half = LANES // 2, HD // 2
        upper = lane >= wide
        inner = jnp.where(upper, lane - wide, lane)
        target = jnp.where(inner < half, inner + jnp.where(upper, half, 0), -columns - LANES * 64)
    else:
        target = jnp.where(lane < HD, lane, -columns - LANES * 64)
    return jnp.where(target + head * HD == column, 1.0, 0.0).astype(jnp.bfloat16)


def dot(left, right, dims):
    return lax.dot_general(left, right, (dims, ((), ())), preferred_element_type=jnp.float32)


NN, NT, TN = ((1,), (0,)), ((1,), (1,)), ((0,), (0,))


def whole(shape):
    return pl.BlockSpec(shape, lambda *_: (0,) * len(shape), pipeline_mode=pl.Buffered(1))


def params(mebibytes, grid=True):
    return pltpu.CompilerParams(
        dimension_semantics=("arbitrary",) if grid else None,
        vmem_limit_bytes=mebibytes * 1024 * 1024,
    )


def cost(flops, moved, exps=0):
    return pl.CostEstimate(flops=int(flops), bytes_accessed=int(moved), transcendentals=int(exps))


def softmax_block(query, keys, block, step, span):
    scores = dot(query, keys, NT) * HD ** (-0.5)
    row = lax.broadcasted_iota(jnp.int32, scores.shape, 0)
    row = jnp.where(row >= step, row - step, row) + block * step
    column = lax.broadcasted_iota(jnp.int32, scores.shape, 1) + span
    scores = jnp.where(row >= column, scores, -jnp.inf)
    exponent = jnp.exp(scores - jnp.max(scores, axis=1, keepdims=True))
    return exponent * (1.0 / jnp.sum(exponent, axis=1, keepdims=True))


def turn(value, cosine, sine):
    return value * cosine + pltpu.roll(value, LANES // 2, 1) * sine


def unturn(value, cosine, sine):
    return value * cosine + pltpu.roll(value * sine, LANES // 2, 1)


def turn_kernel(pairs, qkv, cosine, sine, q_out, k_out, v_out):
    cos, sin = cosine[...], sine[...]
    for h in range(2 * pairs):
        q_out[:, h * LANES : (h + 1) * LANES] = turn(
            qkv[:, h * LANES : (h + 1) * LANES], cos, sin
        ).astype(jnp.bfloat16)
    for g in range(pairs):
        at = (2 * pairs + g) * LANES
        k_out[:, g * LANES : (g + 1) * LANES] = turn(
            qkv[:, at : at + LANES], cos, sin
        ).astype(jnp.bfloat16)
    at = 3 * pairs * LANES
    v_out[...] = qkv[:, at : at + pairs * LANES].astype(jnp.bfloat16)


def attend_kernel(pairs, step, part, *refs):
    heads_out, flat_out = refs[-5:-3] if part == 0 else refs[-2:]
    if part == 0:
        turn_kernel(pairs, *refs[:3], *refs[-3:])
        q, k, v = refs[-3:]
    else:
        q, k, v = refs[:3]
    rows = q.shape[0]
    low = part * (rows // 2)
    for g in range(pairs):
        kv = slice(g * LANES, (g + 1) * LANES)
        for block in range(low // step, (low + rows // 2) // step):
            here = slice(block * step, (block + 1) * step)
            there = slice(block * step - low, (block + 1) * step - low)
            start = (block * step) // L * L
            past = slice(start, (block + 1) * step)
            one, two = (slice((2 * g + e) * LANES, (2 * g + e + 1) * LANES) for e in range(2))
            query = jnp.concatenate([q[here, one], q[here, two]], axis=0)
            prob = softmax_block(query, k[past, kv], block, step, start).astype(jnp.bfloat16)
            result = dot(prob, v[past, kv], NN).astype(jnp.bfloat16)
            heads_out[there, one] = result[:step]
            heads_out[there, two] = result[step:]
    flat = sum(
        dot(heads_out[:, h * LANES : (h + 1) * LANES], selection(2 * pairs * HD, h, False), NN)
        for h in range(2 * pairs)
    )
    flat_out[...] = flat.astype(jnp.bfloat16)


def attend(inputs, pairs, step, part):
    rows = inputs[0].shape[0]
    shapes = [(rows // 2, 2 * pairs * LANES), (rows // 2, 2 * pairs * HD)]
    if part == 0:
        shapes += [(rows, 2 * pairs * LANES), (rows, pairs * LANES), (rows, pairs * LANES)]
    area = rows * min(rows, L) * 2 * pairs * (3 + 4 * part) // 16
    return pl.pallas_call(
        functools.partial(attend_kernel, pairs, step, part),
        out_shape=[jax.ShapeDtypeStruct(shape, jnp.bfloat16) for shape in shapes],
        compiler_params=params(26, False),
        cost_estimate=cost(4 * area * LANES, 10 * inputs[0].size, area),
        name="attend",
    )(*inputs)


def attend_back_kernel(pairs, step, group, *refs):
    q, k, v, low, high, dheads, cosine, sine = refs[:8]
    out, dk, dv, dq = refs[-4:]
    rows = cosine.shape[0]
    cos, sin = cosine[...], sine[...]
    scale = HD ** (-0.5)
    width = 2 * pairs * HD
    flat_q = jnp.zeros((rows, width), jnp.float32)
    flat_kv = jnp.zeros((rows, width), jnp.float32)
    if len(refs) > 12:
        flat_q += refs[8][:, :width].astype(jnp.float32)
        flat_kv += refs[8][:, width:].astype(jnp.float32)
    for g in (group,):
        kv = slice(g * LANES, (g + 1) * LANES)
        dk[...] = jnp.zeros_like(dk)
        dv[...] = jnp.zeros_like(dv)
        for block in range(rows // step):
            here = slice(block * step, (block + 1) * step)
            start = (block * step) // L * L
            past = slice(start, (block + 1) * step)
            one, two = (slice((2 * g + e) * LANES, (2 * g + e + 1) * LANES) for e in range(2))

            def both(ref, at):
                return jnp.concatenate([ref[at, one], ref[at, two]], axis=0)

            query, dhead = both(q, here), both(dheads, here)
            upper = 2 * block * step >= rows
            first = block * step - (rows // 2 if upper else 0)
            head = both(high if upper else low, slice(first, first + step))
            prob = softmax_block(query, k[past, kv], block, step, start)
            dv[past] += dot(prob.astype(jnp.bfloat16), dhead, TN)
            delta = jnp.sum(
                dhead.astype(jnp.float32) * head.astype(jnp.float32), axis=1, keepdims=True
            )
            dscore = (prob * (dot(dhead, v[past, kv], NT) - delta)).astype(jnp.bfloat16)
            dk[past] += dot(dscore, query, TN)
            dquery = dot(dscore, k[past, kv], NN)
            dq[0, here] = dquery[:step]
            dq[1, here] = dquery[step:]
        for e in range(2):
            back = unturn(dq[e] * scale, cos, sin).astype(jnp.bfloat16)
            flat_q += dot(back, selection(width, 2 * g + e, True), NN)
        back = unturn(dk[...] * scale, cos, sin).astype(jnp.bfloat16)
        flat_kv += dot(back, selection(width, g, True), NN)
        flat_kv += dot(dv[...].astype(jnp.bfloat16), selection(width, pairs + g, False), NN)
    out[:, :width] = flat_q.astype(jnp.bfloat16)
    out[:, width:] = flat_kv.astype(jnp.bfloat16)


def attend_back(q, k, v, low, high, dheads, cosine, sine, pairs, step, group, before):
    rows = q.shape[0]
    area = rows * min(rows, L) * 2 * 5 // 8
    held = [] if before is None else [before]
    return pl.pallas_call(
        functools.partial(attend_back_kernel, pairs, step, group),
        out_shape=jax.ShapeDtypeStruct((rows, 4 * pairs * HD), jnp.bfloat16),
        scratch_shapes=[
            pltpu.VMEM((rows, LANES), jnp.float32),
            pltpu.VMEM((rows, LANES), jnp.float32),
            pltpu.VMEM((2, rows, LANES), jnp.float32),
        ],
        compiler_params=params(26, False),
        cost_estimate=cost(10 * area * LANES, 10 * q.size, area),
        name="attend_back",
    )(q, k, v, low, high, dheads, cosine, sine, *held)


def place_kernel(count, me, *refs):
    for k in range(count):

        @pl.when(pl.program_id(0) == k)
        def _(k=k):
            refs[count][...] = refs[k][...]


def place(blocks, me):
    rows, columns = blocks[0].shape
    count = len(blocks)
    return pl.pallas_call(
        functools.partial(place_kernel, count),
        out_shape=jax.ShapeDtypeStruct((count * rows, columns), blocks[0].dtype),
        grid_spec=pltpu.PrefetchScalarGridSpec(
            num_scalar_prefetch=1,
            grid=(count,),
            in_specs=[whole((rows, columns))] * count,
            out_specs=pl.BlockSpec((rows, columns), lambda s, m: (m[0] ^ s, 0)),
        ),
        compiler_params=params(12),
        cost_estimate=cost(0, 4 * count * rows * columns),
        name="place",
    )(me, *blocks)


def norm_place_kernel(count, me, gain, *refs):
    for k in range(count):

        @pl.when(pl.program_id(0) == k)
        def _(k=k):
            refs[count + 1][...] = refs[k][...]
            value = refs[k][...].astype(jnp.float32)
            recip = lax.rsqrt(jnp.mean(value * value, axis=-1, keepdims=True) + EPS)
            refs[count][...] = (value * recip * gain[...]).astype(jnp.bfloat16)


def norm_place(blocks, gain, me):
    rows, columns = blocks[0].shape
    count = len(blocks)
    spot = pl.BlockSpec((rows, columns), lambda s, m: (m[0] ^ s, 0))
    return pl.pallas_call(
        functools.partial(norm_place_kernel, count),
        out_shape=[jax.ShapeDtypeStruct((count * rows, columns), jnp.bfloat16)] * 2,
        grid_spec=pltpu.PrefetchScalarGridSpec(
            num_scalar_prefetch=1,
            grid=(count,),
            in_specs=[whole((1, columns))] + [whole((rows, columns))] * count,
            out_specs=[spot, spot],
        ),
        compiler_params=params(14),
        cost_estimate=cost(0, 6 * count * rows * columns),
        name="norm_place",
    )(me, gain[None, :], *blocks)


def project_kernel(count, kinds, part, info, inputs, gain, *refs):
    attended, weights = refs[:count], refs[count : count + len(kinds)]
    normed, own, joined = refs[-3:]
    here = pl.program_id(0)

    @pl.when(here == 0)
    def _():
        for weight, (base, kind) in zip(weights, kinds):
            depth = weight.shape[0]
            if kind:
                shift = info[1] if kind == 1 else 1 - info[1]
                base = pl.multiple_of(base + shift * depth, 16)
            joined[pl.ds(base, depth)] = weight[...]
        if part:
            own[...] = refs[count + len(kinds) + 1][...]

    features = jnp.concatenate([a[...] for a in attended], axis=1)
    value = inputs[...].astype(jnp.float32) + dot(features, joined[...], NN)
    recip = lax.rsqrt(jnp.mean(value * value, axis=-1, keepdims=True) + EPS)
    normed[...] = (value * recip * gain[...]).astype(jnp.bfloat16)

    @pl.when(here + part * pl.num_programs(0) == info[0])
    def _():
        own[...] = value


def project(inputs, gain, attended, weights, info, part, before):
    count = len(attended)
    rows_all, columns = inputs.shape
    rows, steps = rows_all // count, count // 2
    depth = attended[0].shape[1]
    mine = pl.BlockSpec((rows, columns), lambda s, m: (s + part * steps, 0))
    own = pl.BlockSpec((rows, columns), lambda s, m: (0, 0))
    held = [] if before is None else list(before)
    kinds = [kind for _, kind in weights]
    place_of = 3 + count + len(weights)
    return pl.pallas_call(
        functools.partial(project_kernel, count, kinds, part),
        out_shape=[
            jax.ShapeDtypeStruct((rows_all, columns), jnp.bfloat16),
            jax.ShapeDtypeStruct((rows, columns), jnp.float32),
        ],
        grid_spec=pltpu.PrefetchScalarGridSpec(
            num_scalar_prefetch=1,
            grid=(steps,),
            in_specs=[mine, whole((1, columns))]
            + [pl.BlockSpec((rows, depth), lambda s, m: (s, 0))] * count
            + [whole(weight.shape) for weight, _ in weights]
            + ([pl.BlockSpec(memory_space=pl.ANY), whole((rows, columns))] if held else []),
            out_specs=[mine, own],
            scratch_shapes=[pltpu.VMEM((count * depth, columns), jnp.bfloat16)],
        ),
        input_output_aliases={place_of: 0} if held else {},
        compiler_params=params(40),
        cost_estimate=cost(
            rows_all * depth * count * columns, 3 * inputs.size + 2 * count * depth * columns
        ),
        name="project",
    )(info, inputs, gain[None, :], *attended, *[weight for weight, _ in weights], *held)


def swap(value, axis, size, bit):
    return lax.ppermute(value, axis, [(i, i ^ bit) for i in range(size)])


def gather_blocks(block, size):
    blocks = [block]
    for j in range(1, size):
        low = j & -j
        blocks.append(swap(blocks[j ^ low], "tensor", size, low))
    return blocks


def gather_weight(weight, size, dp):
    far, rows = size // 2, weight.shape[0]
    blocks = {0: [(weight, 0)]}
    if dp % 2 == 0 and size >= 4:
        half = rows // 2
        side = lax.axis_index("dp") & 1
        part = lax.dynamic_slice(weight, (side * half, 0), (half, weight.shape[1]))
        part = swap(part, "tensor", size, far)
        blocks[far] = [(part, 1), (swap(part, "dp", dp, 1), 2)]
    for j in range(1, size):
        if j not in blocks:
            low = j & -j
            blocks[j] = [
                (swap(piece, "tensor", size, low), kind) for piece, kind in blocks[j ^ low]
            ]
    return [(piece, (j * rows, kind)) for j in range(size) for piece, kind in blocks[j]]


def scatter_sum(array, size, me):
    rows = array.shape[0] // size
    parts = {
        j: lax.dynamic_slice(array, ((me ^ j) * rows, 0), (rows, array.shape[1]))
        for j in range(size)
    }
    bit = 1
    while bit < size:
        halves = {}
        for j in reversed(range(0, size, 2 * bit)):
            sent = swap(parts[j ^ bit].astype(jnp.bfloat16), "tensor", size, bit)
            halves[j] = parts[j].astype(jnp.float32) + sent.astype(jnp.float32)
        parts = halves
        bit *= 2
    return parts[0]


def after(value, *others):
    return lax.optimization_barrier((value, *others))[0]


def ring_order(size):
    return list(range(0, size, 2)) + list(reversed(range(1, size, 2)))


def slices_of(main, side, size, width):
    spans = [(0, main[0] // size, c) for c in range(0, main[1], width)]
    spans += [(1, side[0] // size, c) for c in range(0, side[1] // 2, width)]
    return spans, sum(span[1] for span in spans)


def pack_kernel(spans, width, start, main, side, out):
    at = 0
    for which, rows, column in spans:
        out[at : at + rows] = (main, side)[which][:, column : column + width]
        at += rows


def pack(main, side, half, start, sign, width, size):
    spans, depth = slices_of(main.shape, side.shape, size, width)

    def chunk(s, m):
        return lax.rem(m[0] + 2 * size - sign * (1 + s), size)

    return pl.pallas_call(
        functools.partial(pack_kernel, spans, width),
        out_shape=jax.ShapeDtypeStruct((size * depth, width), jnp.bfloat16),
        grid_spec=pltpu.PrefetchScalarGridSpec(
            num_scalar_prefetch=1,
            grid=(size,),
            in_specs=[
                pl.BlockSpec((main.shape[0] // size, main.shape[1]), lambda s, m: (chunk(s, m), 0)),
                pl.BlockSpec(
                    (side.shape[0] // size, side.shape[1] // 2), lambda s, m: (chunk(s, m), half)
                ),
            ],
            out_specs=pl.BlockSpec((depth, width), lambda s, m: (s, 0)),
        ),
        compiler_params=params(8),
        cost_estimate=cost(0, 4 * size * depth * width),
        name="pack",
    )(start, main, side)


def unpack_kernel(spans, width, count, start, *refs):
    pieces, outs = refs[: 2 * count], refs[-3:]
    for k in range(2 * count):

        @pl.when(pl.program_id(0) == k)
        def _(k=k):
            way, at = k // count, 0
            for which, rows, column in spans[way]:
                target = outs[2] if which else outs[way]
                value = pieces[k][at : at + rows].astype(jnp.float32)
                target[:, column : column + width] = value
                at += rows


def unpack(pieces, shapes, start, first, totals, width, size):
    spans = [slices_of(shape, shapes[2], size, width) for shape in shapes[:2]]
    depth = spans[0][1]
    count = len(pieces) // 2

    def forward(s, m):
        step = jnp.minimum(s, count - 1) + first
        return (lax.rem(m[0] + size - step, size), 0)

    def backward(s, m):
        step = jnp.maximum(s - count, 0) + first
        return (lax.rem(m[0] + step, size), 0)

    def beside(s, m):
        turned = s >= count
        chunk = jnp.where(turned, m[0] + s - count + first, m[0] + size - s - first)
        return (lax.rem(chunk, size), jnp.where(turned, 1, 0))

    held = [] if totals is None else list(totals)
    (rows_a, cols_a), (rows_b, cols_b), (rows_c, cols_c) = shapes
    return pl.pallas_call(
        functools.partial(unpack_kernel, [span[0] for span in spans], width, count),
        out_shape=[jax.ShapeDtypeStruct(shape, jnp.float32) for shape in shapes],
        grid_spec=pltpu.PrefetchScalarGridSpec(
            num_scalar_prefetch=1,
            grid=(2 * count,),
            in_specs=[whole((depth, width))] * (2 * count)
            + [pl.BlockSpec(memory_space=pl.ANY)] * len(held),
            out_specs=[
                pl.BlockSpec((rows_a // size, cols_a), forward),
                pl.BlockSpec((rows_b // size, cols_b), backward),
                pl.BlockSpec((rows_c // size, cols_c // 2), beside),
            ],
        ),
        input_output_aliases={1 + 2 * count + k: k for k in range(len(held))},
        compiler_params=params(56),
        cost_estimate=cost(0, 12 * count * depth * width),
        name="unpack",
    )(start, *pieces, *held)


def ring_sum(first, second, side, width, size):
    if size > 8:
        summed = lax.psum((first, second, side), "dp")
        return [total.astype(jnp.float32) for total in summed]
    order = ring_order(size)
    position = [0] * size
    for index, member in enumerate(order):
        position[member] = index
    start = jnp.array(position, jnp.int32)[lax.axis_index("dp")][None]
    hops = {
        sign: [(order[i], order[(i + sign) % size]) for i in range(size)] for sign in (1, -1)
    }

    def hop(k, value):
        return lax.ppermute(value, "dp", hops[(1, -1)[k]])

    packed = [
        pack(main, side, k, start, (1, -1)[k], width, size) for k, main in enumerate((first, second))
    ]
    depth = packed[0].shape[0] // size
    held = [array[:depth] for array in packed]
    for step in range(1, size):
        for k in range(2):
            moved = hop(k, held[k]).astype(jnp.float32)
            mine = packed[k][step * depth : (step + 1) * depth].astype(jnp.float32)
            held[k] = (moved + mine).astype(jnp.bfloat16)
    pieces = [[held[0]], [held[1]]]
    for _ in range(1, size):
        for k in range(2):
            pieces[k].append(hop(k, pieces[k][-1]))
    shapes = (first.shape, second.shape, side.shape)
    totals, low = None, 0
    for high in sorted({size // 2, size - 2, size - 1, size} - {0}):
        if high > low:
            some = pieces[0][low:high] + pieces[1][low:high]
            totals = unpack(some, shapes, start, low, totals, width, size)
            low = high
    return totals


def cross_sum(value, size, axis):
    if size & (size - 1) == 0:
        bit = 1
        while bit < size:
            value = value + swap(value, axis, size, bit)
            bit *= 2
        return value
    return lax.psum(value, axis)


def norm_backward(inputs, gain, dnormed):
    recip = lax.rsqrt(jnp.mean(inputs * inputs, axis=-1, keepdims=True) + EPS)
    scaled = gain * dnormed
    gain_part = jnp.sum(dnormed * inputs * recip, axis=0)
    inner = jnp.mean(scaled * inputs, axis=-1, keepdims=True)
    return (gain_part, recip * scaled - inputs * recip * recip * recip * inner)


def make_body(dp, tensor):
    def layer(
        block_input,
        gain_attention,
        gain_feedforward,
        w_query,
        w_key,
        w_value,
        w_output,
        w_gate,
        w_up,
        w_down,
        cotangent,
    ):
        pair_cols = w_key.shape[1]
        pairs = pair_cols // HD
        rows = block_input.shape[0]
        step = 256
        me = lax.axis_index("tensor")
        spot = me[None].astype(jnp.int32)
        cosine, sine = rope_tables(rows * tensor)
        w_padded = jnp.concatenate(
            [pad_halves(w_query), pad_halves(w_key), pad_heads(w_value)], axis=1
        )
        w_both = jnp.concatenate([w_key.T, w_value.T], axis=0)
        w_output_padded = pad_head_rows(w_output)

        blocks = gather_blocks(block_input, tensor)
        full_one, full_inputs = norm_place(blocks, gain_attention, spot)
        weights = gather_weight(after(w_output, blocks[-1]), tensor, dp)
        qkv = dot(full_one, w_padded, NN)
        low, flat_low, q, k, v = attend((qkv, cosine, sine), pairs, step, 0)
        high, flat_high = attend((q, k, v), pairs, step, 1)
        heads = (low, high)
        attended_low = gather_blocks(flat_low, tensor)
        attended = gather_blocks(flat_high, tensor)
        info = jnp.stack([me, lax.axis_index("dp") & 1]).astype(jnp.int32)
        halves = project(full_inputs, gain_feedforward, attended_low, weights, info, 0, None)
        full_two, resid = project(full_inputs, gain_feedforward, attended, weights, info, 1, halves)
        flat = jnp.concatenate([flat_low, flat_high], axis=0)
        full_grad = place(gather_blocks(after(cotangent, attended[-1]), tensor), spot)

        gate = dot(full_two, w_gate, NN)
        up_proj = dot(full_two, w_up, NN)
        sigmoid_gate = jax.nn.sigmoid(gate)
        activated = gate * sigmoid_gate
        hidden = (activated * up_proj).astype(jnp.bfloat16)
        grad_down = dot(hidden, full_grad, TN).astype(jnp.bfloat16)
        dhidden = dot(full_grad, w_down, NT)
        dgate = (dhidden * up_proj * sigmoid_gate * (1.0 + gate * (1.0 - sigmoid_gate))).astype(
            jnp.bfloat16
        )
        dup_proj = (dhidden * activated).astype(jnp.bfloat16)
        grad_gate = dot(full_two, dgate, TN).astype(jnp.bfloat16)
        grad_up = dot(full_two, dup_proj, TN).astype(jnp.bfloat16)
        total_gate, total_up, total_down = ring_sum(grad_gate, grad_up, grad_down, 256, dp)
        dgate, dup_proj = lax.optimization_barrier((dgate, dup_proj, grad_gate, grad_up, grad_down))[:2]
        dnormed_two = (dot(dgate, w_gate, NT) + dot(dup_proj, w_up, NT)).astype(jnp.bfloat16)
        dnormed_two = scatter_sum(dnormed_two, tensor, me)
        gain_two_part, dresid_norm = norm_backward(resid, gain_feedforward, dnormed_two)
        dresid = cotangent.astype(jnp.float32) + dresid_norm
        full_dresid = place(gather_blocks(dresid.astype(jnp.bfloat16), tensor), spot)
        late_hidden = after(hidden, full_dresid)
        block_output = (
            resid
            + scatter_sum(dot(late_hidden, w_down, NN).astype(jnp.bfloat16), tensor, me)
        ).astype(jnp.bfloat16)
        dheads = dot(full_dresid, w_output_padded, NT).astype(jnp.bfloat16)
        dqkv = None
        for group in range(pairs):
            dqkv = attend_back(
                q, k, v, *heads, dheads, cosine, sine, pairs, step, group, dqkv
            )
        grad_output = dot(flat, full_dresid, TN).astype(jnp.bfloat16)
        dquery, dboth = dqkv[:, : 2 * pair_cols], dqkv[:, 2 * pair_cols :]
        grad_query = dot(full_one, dquery, TN).astype(jnp.bfloat16)
        grad_both = dot(dboth, full_one, TN).astype(jnp.bfloat16)
        total_query, total_both, total_output = ring_sum(
            grad_query, grad_both, grad_output, w_query.shape[1], dp
        )
        dnormed_one = scatter_sum(
            (dot(dquery, w_query, NT) + dot(dboth, w_both, NN)).astype(jnp.bfloat16), tensor, me
        )
        gain_one_part, dinput_norm = norm_backward(
            block_input.astype(jnp.float32), gain_attention, dnormed_one
        )
        input_grad = (dresid + dinput_norm).astype(jnp.bfloat16)
        gains = jnp.stack([gain_one_part, gain_two_part])
        gains = cross_sum(cross_sum(gains, tensor, "tensor"), dp, "dp")
        return (
            block_output,
            input_grad,
            gains[0],
            gains[1],
            total_query,
            total_both[:pair_cols].T,
            total_both[pair_cols:].T,
            total_output,
            total_gate,
            total_up,
            total_down,
        )

    return layer


def solution(mesh):
    placed = (
        P(("dp", "tensor"), None),
        P(),
        P(),
        P(None, "tensor"),
        P(None, "tensor"),
        P(None, "tensor"),
        P("tensor", None),
        P(None, "tensor"),
        P(None, "tensor"),
        P("tensor", None),
        P(("dp", "tensor"), None),
    )
    return jax.shard_map(
        make_body(mesh.shape["dp"], mesh.shape["tensor"]),
        mesh=mesh,
        in_specs=placed,
        out_specs=(
            P(("dp", "tensor"), None),
            P(("dp", "tensor"), None),
            P(),
            P(),
            P(None, "tensor"),
            P(None, "tensor"),
            P(None, "tensor"),
            P("tensor", None),
            P(None, "tensor"),
            P(None, "tensor"),
            P("tensor", None),
        ),
        check_vma=False,
    )
```
